32 devices in a mesh: ep: 32 (over z, y, x, core).
Axes of the slice: x: 2, y: 2, z: 4, core: 2. Of those that a mesh axis runs over, the one named last changes fastest.
Arguments:
- hidden: bfloat16 [32768, 1536], P('ep')
- grad_out: bfloat16 [32768, 1536], P('ep')
- w_router: bfloat16 [1536, 64], replicated
- b_router: float32 [64], replicated
- expert_ids: int32 [32768, 6], P('ep')
- slot_ids: int32 [32768, 6], P('ep')
- w_gate_up: bfloat16 [64, 1536, 1024], P('ep')
- b_gate_up: float32 [64, 1024], P('ep')
- w_down: bfloat16 [64, 512, 1536], P('ep')
- b_down: float32 [64, 1536], P('ep')
Outputs:
- output 1: bfloat16 [32768, 1536], P('ep')
- output 2: bfloat16 [32768, 1536], P('ep')
- output 3: float32 [1536, 64], replicated
- output 4: float32 [64], replicated
- output 5: float32 [64, 1536, 1024], P('ep')
- output 6: float32 [64, 1024], P('ep')
- output 7: float32 [64, 512, 1536], P('ep')
- output 8: float32 [64, 1536], P('ep')
All inputs are finite; a program needn't handle non-finite values.
Results may differ from the reference program's by a relative error of at most 0.00506232.
Values are sent between devices in bfloat16 or wider.
A program may use at most 1 GiB of HBM per device.

```python
import jax
import jax.numpy as jnp
from jax import lax

D_MODEL = 1536
FF_EXPERT = 512
EXPERTS = 64
TOP_K = 6
TOKENS_DEV = 1024
EP_DEVICES = 32

TOKENS = EP_DEVICES * TOKENS_DEV
CAPACITY = (3 * TOKENS_DEV * TOP_K + 2 * EXPERTS - 1) // (2 * EXPERTS)
ROWS_EXPERT = EP_DEVICES * CAPACITY
SWIGLU_LIMIT = 7.0
SWIGLU_ALPHA = 1.702


def draw_routing(key):
    key_bias, key_dev = jax.random.split(key)
    expert_bias = jax.random.randint(key_bias, (EXPERTS,), 0, 512)
    expert_range = jnp.arange(EXPERTS, dtype=jnp.int32)
    copies = TOKENS_DEV * TOP_K

    def one_device(dev_key):
        key_noise, key_hot, key_pick, key_prio = jax.random.split(dev_key, 4)
        noise_int = jax.random.randint(key_noise, (TOKENS_DEV, EXPERTS), 0, 1024)
        hot_expert = jax.random.randint(key_hot, (), 0, EXPERTS)
        forced = jax.random.permutation(key_pick, TOKENS_DEV) < 2 * CAPACITY
        hot_bonus = jnp.where(forced[:, None] & (expert_range[None, :] == hot_expert), 4096, 0)
        scores = (noise_int + expert_bias[None, :] + hot_bonus) * EXPERTS + expert_range[None, :]
        choice = lax.top_k(scores, TOP_K)[1].astype(jnp.int32)
        flat_ids = choice.reshape(-1)
        priority = jax.random.permutation(key_prio, copies)
        sort_order = jnp.argsort(flat_ids * copies + priority)
        counts = jnp.bincount(flat_ids, length=EXPERTS)
        starts = jnp.cumsum(counts) - counts
        rank_sorted = (jnp.arange(copies, dtype=jnp.int32) - starts[flat_ids[sort_order]]).astype(jnp.int32)
        slot_rank = jnp.zeros((copies,), jnp.int32).at[sort_order].set(rank_sorted)
        slot_ids = jnp.where(slot_rank < CAPACITY, slot_rank, -1).reshape(TOKENS_DEV, TOP_K)
        return choice, slot_ids

    choice, slot_ids = jax.vmap(one_device)(jax.random.split(key_dev, EP_DEVICES))
    return choice.reshape(TOKENS, TOP_K), slot_ids.reshape(TOKENS, TOP_K).astype(jnp.int32)


def setup_inputs(seed: int = 0) -> dict:
    key_list = jax.random.split(jax.random.key(seed), 9)
    hidden = jax.random.normal(key_list[0], (TOKENS, D_MODEL), jnp.float32).astype(jnp.bfloat16)
    grad_out = jax.random.normal(key_list[1], (TOKENS, D_MODEL), jnp.float32).astype(jnp.bfloat16)
    w_router = (2.0 * D_MODEL ** -0.5 * jax.random.normal(key_list[2], (D_MODEL, EXPERTS), jnp.float32)).astype(jnp.bfloat16)
    b_router = jax.random.normal(key_list[3], (EXPERTS,), jnp.float32)
    expert_ids, slot_ids = draw_routing(key_list[4])
    w_gate_up = (3.0 * D_MODEL ** -0.5 * jax.random.normal(key_list[5], (EXPERTS, D_MODEL, 2 * FF_EXPERT), jnp.float32)).astype(jnp.bfloat16)
    b_gate_up = jax.random.normal(key_list[6], (EXPERTS, 2 * FF_EXPERT), jnp.float32)
    w_down = (0.15 * FF_EXPERT ** -0.5 * jax.random.normal(key_list[7], (EXPERTS, FF_EXPERT, D_MODEL), jnp.float32)).astype(jnp.bfloat16)
    b_down = 0.5 * jax.random.normal(key_list[8], (EXPERTS, D_MODEL), jnp.float32)
    return {'hidden': hidden, 'grad_out': grad_out, 'w_router': w_router, 'b_router': b_router, 'expert_ids': expert_ids, 'slot_ids': slot_ids, 'w_gate_up': w_gate_up, 'b_gate_up': b_gate_up, 'w_down': w_down, 'b_down': b_down}


def swiglu(pre_act):
    col_pairs = pre_act.reshape(pre_act.shape[:-1] + (pre_act.shape[-1] // 2, 2))
    gate_in = jnp.minimum(col_pairs[..., 0], SWIGLU_LIMIT)
    up_in = jnp.clip(col_pairs[..., 1], -SWIGLU_LIMIT, SWIGLU_LIMIT)
    return gate_in * jax.nn.sigmoid(SWIGLU_ALPHA * gate_in) * (up_in + 1.0)


def reference(hidden, grad_out, w_router, b_router, expert_ids, slot_ids, w_gate_up, b_gate_up, w_down, b_down):
    buf_total = EXPERTS * ROWS_EXPERT
    copy_count = TOKENS * TOP_K
    src_dev = (jnp.arange(TOKENS, dtype=jnp.int32) // TOKENS_DEV)[:, None]
    dest_row = jnp.where(slot_ids >= 0, expert_ids * ROWS_EXPERT + src_dev * CAPACITY + slot_ids, buf_total)
    src_copy = jnp.full((buf_total + 1,), copy_count, jnp.int32).at[dest_row.reshape(-1)].set(jnp.arange(copy_count, dtype=jnp.int32))[:buf_total].reshape(EXPERTS, ROWS_EXPERT)
    logits = jnp.dot(hidden, w_router, preferred_element_type=jnp.float32) + b_router
    gate_w = jax.nn.softmax(jnp.take_along_axis(logits, expert_ids, axis=1), axis=-1)
    flat_gate = gate_w.reshape(-1)

    def expert_forward(expert_args):
        w_gu, b_gu, w_dn, b_dn, src_rows = expert_args
        x_rows = jnp.take(hidden, src_rows // TOP_K, axis=0, mode='fill', fill_value=0)
        pre_act = jnp.dot(x_rows, w_gu, preferred_element_type=jnp.float32) + b_gu
        act_bf = swiglu(pre_act).astype(jnp.bfloat16)
        return (jnp.dot(act_bf, w_dn, preferred_element_type=jnp.float32) + b_dn).astype(jnp.bfloat16)

    y_flat = lax.map(expert_forward, (w_gate_up, b_gate_up, w_down, b_down, src_copy)).reshape(buf_total, D_MODEL)

    def token_forward(block_args):
        gate_blk, dest_blk, grad_blk = block_args
        y_blk = jnp.take(y_flat, dest_blk, axis=0, mode='fill', fill_value=0).astype(jnp.float32)
        out_blk = jnp.sum(gate_blk[:, :, None] * y_blk, axis=1).astype(jnp.bfloat16)
        return out_blk, jnp.einsum('td,tkd->tk', grad_blk.astype(jnp.float32), y_blk)

    dev_shape = (EP_DEVICES, TOKENS_DEV)
    block_out, gate_grad = lax.map(token_forward, (gate_w.reshape(dev_shape + (TOP_K,)), dest_row.reshape(dev_shape + (TOP_K,)), grad_out.reshape(dev_shape + (D_MODEL,))))
    block_out = block_out.reshape(TOKENS, D_MODEL)
    gate_grad = gate_grad.reshape(TOKENS, TOP_K)
    sel_grad = gate_w * (gate_grad - jnp.sum(gate_w * gate_grad, axis=1, keepdims=True))
    logit_grad = jnp.zeros((TOKENS, EXPERTS), jnp.float32).at[jnp.arange(TOKENS)[:, None], expert_ids].add(sel_grad).astype(jnp.bfloat16)

    def expert_backward(expert_args):
        w_gu, b_gu, w_dn, src_rows = expert_args
        tok_rows = src_rows // TOP_K
        x_rows = jnp.take(hidden, tok_rows, axis=0, mode='fill', fill_value=0)
        pre_act = jnp.dot(x_rows, w_gu, preferred_element_type=jnp.float32) + b_gu
        act_val, act_vjp = jax.vjp(swiglu, pre_act)
        act_bf = act_val.astype(jnp.bfloat16)
        row_gate = jnp.take(flat_gate, src_rows, axis=0, mode='fill', fill_value=0)
        row_grad = jnp.take(grad_out, tok_rows, axis=0, mode='fill', fill_value=0).astype(jnp.float32)
        q_rows = (row_gate[:, None] * row_grad).astype(jnp.bfloat16)
        grad_b_dn = jnp.sum(q_rows.astype(jnp.float32), axis=0)
        grad_w_dn = jnp.dot(act_bf.T, q_rows, preferred_element_type=jnp.float32)
        act_grad = jnp.dot(q_rows, w_dn.T, preferred_element_type=jnp.float32)
        pre_grad = act_vjp(act_grad)[0].astype(jnp.bfloat16)
        grad_b_gu = jnp.sum(pre_grad.astype(jnp.float32), axis=0)
        grad_w_gu = jnp.dot(x_rows.T, pre_grad, preferred_element_type=jnp.float32)
        p_rows = jnp.dot(pre_grad, w_gu.T, preferred_element_type=jnp.float32).astype(jnp.bfloat16)
        return grad_w_gu, grad_b_gu, grad_w_dn, grad_b_dn, p_rows

    grad_w_gate_up, grad_b_gate_up, grad_w_down, grad_b_down, p_rows = lax.map(expert_backward, (w_gate_up, b_gate_up, w_down, src_copy))
    p_flat = p_rows.reshape(buf_total, D_MODEL)

    def token_backward(block_args):
        dest_blk, logit_blk = block_args
        p_blk = jnp.take(p_flat, dest_blk, axis=0, mode='fill', fill_value=0).astype(jnp.float32)
        router_dx = jnp.dot(logit_blk, w_router.T, preferred_element_type=jnp.float32)
        return (jnp.sum(p_blk, axis=1) + router_dx).astype(jnp.bfloat16)

    grad_hidden = lax.map(token_backward, (dest_row.reshape(dev_shape + (TOP_K,)), logit_grad.reshape(dev_shape + (EXPERTS,)))).reshape(TOKENS, D_MODEL)
    grad_w_router = jnp.dot(hidden.T, logit_grad, preferred_element_type=jnp.float32)
    grad_b_router = jnp.sum(logit_grad.astype(jnp.float32), axis=0)
    return (block_out, grad_hidden, grad_w_router, grad_b_router, grad_w_gate_up, grad_b_gate_up, grad_w_down, grad_b_down)
```

```python
import jax
import jax.numpy as jnp
from jax import lax
from jax.sharding import PartitionSpec as P

SWIGLU_LIMIT = 7.0
SWIGLU_ALPHA = 1.702


def gated_act(gate_pre, up_pre):
    gate_in = jnp.minimum(gate_pre, SWIGLU_LIMIT)
    up_in = jnp.clip(up_pre, -SWIGLU_LIMIT, SWIGLU_LIMIT)
    return gate_in * jax.nn.sigmoid(SWIGLU_ALPHA * gate_in) * (up_in + 1.0)


def take_rows(rows, index):
    return rows.at[index].get(mode='promise_in_bounds')


def solution(mesh):
    ep_size = mesh.shape['ep']

    def local_block(hidden, grad_out, w_router, b_router, expert_ids, slot_ids, w_gate_up, b_gate_up, w_down, b_down):
        f32, bf16 = jnp.float32, jnp.bfloat16
        tok_local, d_model = hidden.shape
        top_k = expert_ids.shape[1]
        experts = w_router.shape[1]
        local_experts = w_gate_up.shape[0]
        ff = w_down.shape[1]
        capacity = (3 * tok_local * top_k + 2 * experts - 1) // (2 * experts)
        part_rows = ep_size * capacity
        buf_rows = experts * capacity
        copy_count = tok_local * top_k

        ids_t, slots_t = expert_ids.T, slot_ids.T
        kept = slots_t >= 0
        row_t = (ids_t % local_experts) * part_rows + (ids_t // local_experts) * capacity + slots_t
        dest_row = jnp.where(kept, row_t, buf_rows)
        src_copy = jnp.full((buf_rows + 1,), copy_count, jnp.int32).at[dest_row.reshape(-1)].set(jnp.arange(copy_count, dtype=jnp.int32))[:buf_rows]
        src_tok = jnp.where(src_copy < copy_count, src_copy % tok_local, tok_local)
        back_row = jnp.where(kept, row_t, 0).reshape(-1)

        def exchange(rows):
            return lax.all_to_all(rows, 'ep', 0, 0, tiled=True)

        def part(index, e):
            return lax.slice(index, (e * part_rows,), ((e + 1) * part_rows,))

        hidden_pad = jnp.pad(hidden, ((0, 16), (0, 0)))
        recv_x = [exchange(take_rows(hidden_pad, part(src_tok, e))) for e in range(local_experts)]

        logits = jnp.dot(hidden, w_router, preferred_element_type=f32) + b_router
        expert_range = jnp.arange(experts, dtype=jnp.int32)
        chosen = ids_t[:, :, None] == expert_range
        gate_w = jax.nn.softmax(jnp.sum(jnp.where(chosen, logits[None], 0.0), axis=2), axis=0)
        q_copies = (gate_w[:, :, None] * grad_out[None].astype(f32)).astype(bf16).reshape(copy_count, d_model)
        q_copies = jnp.pad(q_copies, ((0, 16), (0, 0)))

        col = jnp.arange(2 * ff, dtype=jnp.int32)
        split = (col[:, None] == jnp.where(col < ff, 2 * col, 2 * (col - ff) + 1)[None, :]).astype(bf16)
        w_split = [jnp.dot(w_gate_up[e], split, preferred_element_type=f32).astype(bf16) for e in range(local_experts)]

        acts, vjps, back_y = [], [], []
        for e in range(local_experts):
            b_pair = b_gate_up[e].reshape(ff, 2)
            b_split = jnp.concatenate([b_pair[:, 0], b_pair[:, 1]])
            pre_act = jnp.dot(recv_x[e], w_split[e], preferred_element_type=f32) + b_split
            act_val, act_vjp = jax.vjp(gated_act, pre_act[:, :ff], pre_act[:, ff:])
            act_bf = act_val.astype(bf16)
            y_rows = (jnp.dot(act_bf, w_down[e], preferred_element_type=f32) + b_down[e]).astype(bf16)
            acts.append(act_bf)
            vjps.append(act_vjp)
            back_y.append(exchange(y_rows))

        recv_q = [exchange(take_rows(q_copies, part(src_copy, e))) for e in range(local_experts)]

        y_copies = take_rows(jnp.concatenate(back_y), back_row).reshape(top_k, tok_local, d_model)
        y_kept = jnp.where(kept[:, :, None], y_copies, 0).astype(f32)
        block_out = jnp.sum(gate_w[:, :, None] * y_kept, axis=0).astype(bf16)
        gate_grad = jnp.sum(grad_out[None].astype(f32) * y_kept, axis=2)
        sel_grad = gate_w * (gate_grad - jnp.sum(gate_w * gate_grad, axis=0, keepdims=True))
        logit_grad = jnp.sum(jnp.where(chosen, sel_grad[:, :, None], 0.0), axis=0).astype(bf16)
        grad_w_router = lax.psum(jnp.dot(hidden.T, logit_grad, preferred_element_type=f32), 'ep')
        grad_b_router = lax.psum(jnp.sum(logit_grad, axis=0, dtype=f32), 'ep')
        router_dx = jnp.dot(logit_grad, w_router.T, preferred_element_type=f32)

        back_p, pre_grads = [], []
        for e in range(local_experts):
            act_grad = jnp.dot(recv_q[e], w_down[e].T, preferred_element_type=f32)
            gate_d, up_d = vjps[e](act_grad)
            pre_split = jnp.concatenate([gate_d.astype(bf16), up_d.astype(bf16)], axis=1)
            if e == local_experts - 1:
                pre_split, _ = lax.optimization_barrier((pre_split, (logit_grad, block_out)))
            p_rows = jnp.dot(pre_split, w_split[e].T, preferred_element_type=f32).astype(bf16)
            back_p.append(exchange(p_rows))
            pre_grads.append(pre_split)

        g_wd, g_bd, g_wgu, g_bgu = [], [], [], []
        for e in range(local_experts):
            pre_grad = jnp.dot(pre_grads[e], split.T, preferred_element_type=f32).astype(bf16)
            g_bd.append(jnp.sum(recv_q[e], axis=0, dtype=f32))
            g_wd.append(jnp.dot(acts[e].T, recv_q[e], preferred_element_type=f32))
            g_bgu.append(jnp.sum(pre_grad, axis=0, dtype=f32))
            g_wgu.append(jnp.dot(recv_x[e].T, pre_grad, preferred_element_type=f32))

        dx = router_dx
        for e in range(local_experts):
            here = kept & (ids_t % local_experts == e)
            row_e = jnp.where(here, row_t - e * part_rows, 0).reshape(-1)
            p_copies = take_rows(back_p[e], row_e).reshape(top_k, tok_local, d_model)
            dx = dx + jnp.sum(jnp.where(here[:, :, None], p_copies, 0).astype(f32), axis=0)
        grad_hidden = dx.astype(bf16)
        return (block_out, grad_hidden, grad_w_router, grad_b_router, jnp.stack(g_wgu), jnp.stack(g_bgu), jnp.stack(g_wd), jnp.stack(g_bd))

    tok_spec = P('ep', None)
    in_specs = (tok_spec, tok_spec, P(None, None), P(None), tok_spec, tok_spec, P('ep', None, None), P('ep', None), P('ep', None, None), P('ep', None))
    out_specs = (tok_spec, tok_spec, P(None, None), P(None), P('ep', None, None), P('ep', None), P('ep', None, None), P('ep', None))
    return jax.shard_map(local_block, mesh=mesh, in_specs=in_specs, out_specs=out_specs, check_vma=False)
```
